512 devices in a mesh: ctx: 16 (over x_lo, y, core), ep: 32 (over z, x_hi).
Axes of the slice: x: 4 (x_hi: 2, x_lo: 2; x = x_hi * 2 + x_lo), y: 4, z: 16, core: 2. Of those that a mesh axis runs over, the one named last changes fastest.
Arguments:
- queries: bfloat16 [2048, 73728], P('ctx', 'ep'), may hold values from -12 to 12
- latent: bfloat16 [2048, 576], P('ctx'), may hold values from -5 to 5
- doc_ids: int32 [2048], replicated, may hold values from 0 to 3, never falling along the last dimension, each value on 1 to 1024 neighbouring positions
- w_uv: bfloat16 [128, 512, 128], P('ep'), may hold values from -0.75 to 0.75
- w_out: bfloat16 [16384, 7168], P('ep', 'ctx'), may hold values from -0.046875 to 0.046875
- hidden_in: bfloat16 [2048, 7168], P('ep', 'ctx'), may hold values from -24 to 24
- norm_gain: float32 [7168], P('ctx'), may hold values from 0.5 to 1.5
- route_ids: int32 [2048, 8], P('ep'), may hold values from 0 to 31, all different within a row; in each aligned block of 64 rows (0 to 63, 64 to 127, ...) at most 18 rows name the same one
- route_weights: float32 [2048, 8], P('ep'), may hold values from 0.1 to 1
- w_gate: bfloat16 [32, 7168, 1024], P('ep', 'ctx'), may hold values from -0.0625 to 0.0625
- w_up: bfloat16 [32, 7168, 1024], P('ep', 'ctx'), may hold values from -0.0625 to 0.0625
- w_down: bfloat16 [32, 1024, 7168], P('ep', None, 'ctx'), may hold values from -0.1875 to 0.1875
Outputs:
- layer_output: bfloat16 [2048, 7168], P('ep', 'ctx')
The draws below stay inside these ranges and needn't reach their ends.
Inputs may be any that keep to these rules, and one draw needn't show every extreme that they name: `doc_ids`: document numbers never fall along the sequence; a document has at most 1024 tokens, and one has exactly that many. `route_ids`: each token names 8 different experts; among the 64 tokens of one index of ep no expert is named by more than 18 tokens, a bound that some block reaches.
All inputs are finite; a program needn't handle non-finite values.
Results may differ from the reference program's by a relative error of at most 0.014.
Values may be sent and summed in bfloat16 or wider, within the bound.
A program may use at most 64 MiB of HBM per device.

```python
import math
import jax
import jax.numpy as jnp
import numpy as np
from jax import lax

D = 7168
HEADS = 128
KVL = 512
ROPE = 64
VDIM = 128
FF = 1024
TOP = 8
EXPERTS = 32
L = 2048
TOKD = 64
HEADS_DEV = 4
CAP = 18
N_CTX = 16
N_EP = 32


def attention_inputs(key):
    width = KVL + ROPE
    base_key = jax.random.fold_in(key, 4242)
    first, second = jax.random.split(base_key, 2)
    keys_out = jnp.clip(jax.random.normal(first, (L, width), jnp.float32), -4.0, 4.0)
    query_out = 0.5 * jnp.clip(jax.random.normal(second, (L, HEADS, width), jnp.float32), -4.0, 4.0)
    return (query_out.reshape(L, HEADS * width), keys_out)


def draw_queries(key, part):
    return attention_inputs(key)[0].astype(jnp.bfloat16)


def draw_latent(key, part):
    return attention_inputs(key)[1].astype(jnp.bfloat16)


def draw_hidden_in(key, part):
    first = jax.random.fold_in(jax.random.fold_in(key, 77), 0)
    columns = jnp.exp(math.log(3.0) * jnp.arange(D, dtype=jnp.float32) / (D - 1))
    values = jnp.clip(jax.random.normal(first, (L, D), jnp.float32), -4.0, 4.0)
    return (values * columns[None, :]).astype(jnp.bfloat16)


def level_of(stream_key, shape, shards, smallest, high):
    factor_of = 1.0
    for position, shards_of in shards:
        draws = jax.random.uniform(jax.random.fold_in(jax.random.fold_in(stream_key, 6), position), (shards_of,), jnp.float32, smallest / len(shards), high / len(shards))
        factor_of = factor_of * jnp.repeat(jnp.exp(draws), shape[position] // shards_of).reshape((-1,) + (1,) * (len(shape) - 1 - position))
    return factor_of


def profile(count, total, reach, slope):
    portions = [(1 << 20) // math.isqrt(standing ** slope) + 1 for standing in range(2, count + 1)]
    surplus, counts = total - reach - (count - 1), [1] * (count - 1)
    while surplus > 0:
        free = [i for i in range(count - 1) if counts[i] < reach]
        mass, left = sum([portions[i] for i in free]), surplus
        for i in free:
            extra = min(reach - counts[i], max(1, left * portions[i] // mass), surplus)
            counts[i] = counts[i] + extra
            surplus = surplus - extra
    return np.array([reach] + counts)


def ragged(rng, number_of, total, bound, slope):
    if number_of == 2:
        one = jax.random.randint(rng, (), max(1, total - bound), min(bound, total - 1) + 1)
        return jnp.stack([one, total - one])
    tallies = jnp.asarray(profile(number_of, total, bound, slope), jnp.int32)
    couples = (number_of - 1) // 2
    donor, taker = tallies[1:1 + 2 * couples:2], tallies[2:2 + 2 * couples:2]
    slack = jnp.minimum(donor - 1, bound - taker)
    passed = jax.random.randint(jax.random.fold_in(rng, 1), (couples,), 0, 1 << 20) % (slack + 1)
    tallies = tallies.at[1:1 + 2 * couples:2].set(donor - passed).at[2:2 + 2 * couples:2].set(taker + passed)
    return tallies[jax.random.permutation(jax.random.fold_in(rng, 2), number_of)]


def routed_block(rng, own, number, rows, amount, top, limit, slope):
    sequence = jax.random.permutation(rng, amount)
    packed, usual = shares(amount, rows * top, limit, slope, True), shares(amount, rows * top, limit, slope, False)
    places = jnp.arange(amount)

    def named(sizes, turn):
        used = int((sizes > 0).sum())
        fixed = max(1, used // 4)
        moved = fixed + (places - fixed + turn * (used - fixed)) % max(1, amount - fixed)
        return jnp.zeros((amount,), jnp.int32).at[sequence[jnp.where(places < fixed, places, moved)]].set(jnp.asarray(sizes, jnp.int32))

    sizes = jnp.where(number % 4 == 0, named(packed, number // 4), named(usual, number - number // 4 - 1))
    mixed = jax.random.permutation(jax.random.fold_in(own, 3), amount)
    donor, receiver = mixed[0:amount // 2 * 2:2], mixed[1:amount // 2 * 2:2]
    room = jnp.minimum(sizes[donor] - 1, limit - sizes[receiver]) // 2
    room = jnp.where((donor == sequence[0]) | (receiver == sequence[0]) | (sizes[receiver] == 0), 0, jnp.maximum(room, 0))
    moved = jax.random.randint(jax.random.fold_in(own, 4), (amount // 2,), 0, 1 << 20) % (room + 1)
    sizes = sizes.at[donor].add(-moved).at[receiver].add(moved)
    members = jnp.searchsorted(jnp.cumsum(sizes), jnp.arange(rows * top), side="right").astype(jnp.int32)
    grid = members.reshape(top, rows).T
    grid = grid[jax.random.permutation(jax.random.fold_in(own, 1), rows)]
    turn = jax.random.randint(jax.random.fold_in(own, 2), (rows, 1), 0, top)
    return jnp.take_along_axis(grid, (jnp.arange(top)[None, :] + turn) % top, axis=1)


def shares(number_of, total, reach, skew, full):
    portions = [(1 << 20) // math.isqrt(rank ** skew) + 1 for rank in range(1, number_of + 1)]
    largest = reach if full else min(reach, max(-(-total // number_of), total * portions[0] // sum(portions)))
    least = 1 if total - largest >= number_of - 1 else 0
    holding, rest = [largest] + [least] * (number_of - 1), total - largest - least * (number_of - 1)
    while rest > 0:
        free = [i for i in range(1, number_of) if holding[i] < largest] or [i for i in range(1, number_of) if holding[i] < reach]
        mass, remaining = sum([portions[i] for i in free]), rest
        for i in free:
            addition = min(reach - holding[i], max(1, remaining * portions[i] // mass), rest)
            holding[i] = holding[i] + addition
            rest = rest - addition
    return np.array(holding)


def bell_draw(key, shape, deviation, limit, cuts=(), kind=jnp.bfloat16):
    values = jax.random.normal(key, shape, jnp.float32) * deviation
    if len(cuts) > 0:
        values = level_of(key, shape, cuts, -0.22, 0.18) * values
    return jnp.clip(values, min=-limit, max=limit).astype(kind)


def setup_inputs(seed: int = 0) -> dict:
    key_list = jax.random.split(jax.random.key(seed), 13)
    queries = draw_queries(jax.random.fold_in(key_list[12], 71), 0)
    latent = draw_latent(jax.random.fold_in(key_list[12], 71), 0)
    doc_ids = jnp.searchsorted(jnp.cumsum(ragged(key_list[2], 4, L, L // 2, 1)), jnp.arange(L), side="right").astype(jnp.int32)
    w_uv = bell_draw(key_list[3], (HEADS, KVL, VDIM), (KVL // 9) ** -0.5, 0.75, ((0, 32),))
    w_out = bell_draw(key_list[4], (HEADS * VDIM, D), (HEADS * VDIM) ** -0.5, 0.046875, ((0, 32), (1, 16)))
    hidden_in = draw_hidden_in(jax.random.fold_in(key_list[12], 71), 0)
    norm_gain = jnp.clip(1.0 + 0.1 * jax.random.normal(key_list[6], (D,), jnp.float32), 0.5, 1.5)
    route_ids_keys = jax.random.split(jax.random.fold_in(key_list[7], 1), L // TOKD)
    route_ids_turns = jax.random.permutation(jax.random.fold_in(key_list[7], 3), L // TOKD)
    route_ids = jax.vmap(lambda own, number: routed_block(jax.random.fold_in(key_list[7], 2), own, number, TOKD, EXPERTS, TOP, CAP, 2))(route_ids_keys, route_ids_turns).reshape((L, TOP))
    route_weights = jnp.clip(jnp.exp(math.log(1.0) - 2.3025851 * jax.random.uniform(key_list[8], (L, TOP), jnp.float32) ** level_of(key_list[8], (L, TOP), ((0, 32),), -0.2, 0.2)), 0.1, 1.0)
    w_gate = bell_draw(key_list[9], (EXPERTS, D, FF), D ** -0.5, 0.0625, ((0, 32), (1, 16)))
    w_up = bell_draw(key_list[10], (EXPERTS, D, FF), D ** -0.5, 0.0625, ((0, 32), (1, 16)))
    w_down = bell_draw(key_list[11], (EXPERTS, FF, D), FF ** -0.5, 0.1875, ((0, 32), (2, 16)))
    return {"queries": queries, "latent": latent, "doc_ids": doc_ids, "w_uv": w_uv, "w_out": w_out, "hidden_in": hidden_in, "norm_gain": norm_gain, "route_ids": route_ids, "route_weights": route_weights, "w_gate": w_gate, "w_up": w_up, "w_down": w_down}


score_scale = (1.0 + 0.1 * math.log(40.0)) ** 2 / math.sqrt(192.0)
masked_score = -1e+30

def reference(queries, latent, doc_ids, w_uv, w_out, hidden_in, norm_gain, route_ids, route_weights, w_gate, w_up, w_down):
    key_width = KVL + ROPE
    positions = jnp.arange(L, dtype=jnp.int32)
    allowed = (positions[None, :] <= positions[:, None]) & (doc_ids[None, :] == doc_ids[:, None])
    latent_full = latent.astype(jnp.float32)
    values_full = latent_full[:, :KVL]

    def one_group(running, group):
        start = (group * HEADS_DEV * key_width).astype(jnp.int32)
        block = lax.dynamic_slice_in_dim(queries, start, HEADS_DEV * key_width, 1)
        block = block.reshape(L, HEADS_DEV, key_width).astype(jnp.float32)
        scores = jnp.einsum('qhc,kc->hqk', block, latent_full) * score_scale
        scores = jnp.where(allowed[None], scores, masked_score)
        peak = lax.optimization_barrier(jnp.max(scores, axis=2, keepdims=True))
        probs = jnp.where(allowed[None], jnp.exp(scores - peak), 0.0)
        totals = lax.optimization_barrier(jnp.sum(probs, axis=2))
        rounded = lax.optimization_barrier(probs.astype(jnp.bfloat16)).astype(jnp.float32)
        context = (jnp.einsum('hqk,kc->hqc', rounded, values_full) / totals[:, :, None]).astype(jnp.bfloat16)
        head_start = (group * HEADS_DEV).astype(jnp.int32)
        up_weights = lax.dynamic_slice_in_dim(w_uv, head_start, HEADS_DEV, 0).astype(jnp.float32)
        head_values = jnp.einsum('hqc,hcv->qhv', context.astype(jnp.float32), up_weights)
        head_values = head_values.reshape(L, HEADS_DEV * VDIM).astype(jnp.bfloat16)
        row_start = (group * HEADS_DEV * VDIM).astype(jnp.int32)
        out_rows = lax.dynamic_slice_in_dim(w_out, row_start, HEADS_DEV * VDIM, 0)
        partial_value = jnp.dot(head_values, out_rows, preferred_element_type=jnp.float32)
        partial_value = lax.optimization_barrier(partial_value.astype(jnp.bfloat16)).astype(jnp.float32)
        return (running + partial_value, 0)
    attended, unused = lax.scan(one_group, jnp.zeros((L, D), jnp.float32), jnp.arange(N_EP, dtype=jnp.int32))
    residual = hidden_in.astype(jnp.float32) + attended
    normed = residual * lax.rsqrt(lax.optimization_barrier(jnp.mean(residual * residual, axis=1, keepdims=True)) + 1e-06) * norm_gain
    normed = normed.astype(jnp.bfloat16)
    pair_ids = route_ids.reshape(N_EP, TOKD * TOP)
    chosen = (pair_ids[:, :, None] == jnp.arange(EXPERTS, dtype=jnp.int32)[None, None, :]).astype(jnp.int32)
    earlier = jnp.cumsum(chosen, axis=1) - chosen
    slot = lax.optimization_barrier(jnp.sum(earlier * chosen, axis=2))
    sources = jnp.arange(N_EP, dtype=jnp.int32)[:, None]
    where_to = (pair_ids * (N_EP * CAP) + sources * CAP + slot).reshape(-1).astype(jnp.int32)
    owners = (jnp.arange(L * TOP, dtype=jnp.int32) // TOP).astype(jnp.int32)
    table = jnp.full((EXPERTS * N_EP * CAP,), L, jnp.int32).at[where_to].set(owners)
    padded = jnp.concatenate([normed, jnp.zeros((1, D), jnp.bfloat16)], axis=0)

    def one_expert(pieces):
        index, gate_weight, up_weight, down_weight = pieces
        taken = padded[index].reshape(N_EP * CAP, N_CTX, D // N_CTX).astype(jnp.float32)
        gate_parts = jnp.einsum('mcd,cdf->cmf', taken, gate_weight.reshape(N_CTX, D // N_CTX, FF).astype(jnp.float32))
        up_parts = jnp.einsum('mcd,cdf->cmf', taken, up_weight.reshape(N_CTX, D // N_CTX, FF).astype(jnp.float32))
        gate = lax.optimization_barrier(jnp.sum(lax.optimization_barrier(gate_parts.astype(jnp.bfloat16)).astype(jnp.float32), axis=0))
        upper = lax.optimization_barrier(jnp.sum(lax.optimization_barrier(up_parts.astype(jnp.bfloat16)).astype(jnp.float32), axis=0))
        activated = (jax.nn.silu(gate) * upper).astype(jnp.bfloat16)
        return jnp.dot(activated, down_weight, preferred_element_type=jnp.float32).astype(jnp.bfloat16)
    outputs = lax.map(one_expert, (table.reshape(EXPERTS, N_EP * CAP), w_gate, w_up, w_down))
    returned = outputs.reshape(EXPERTS * N_EP * CAP, D)[where_to]
    mixture = lax.optimization_barrier(jnp.sum(returned.astype(jnp.float32).reshape(L, TOP, D) * route_weights[:, :, None], axis=1))
    return (residual + mixture).astype(jnp.bfloat16)
```

```python
import math

import jax
import jax.numpy as jnp
from jax import lax
from jax.experimental import pallas as pl
from jax.experimental.pallas import tpu as pltpu
from jax.sharding import PartitionSpec as P

D = 7168
KVL = 512
KW = 576
HEADS_DEV = 4
VDIM = 128
NX, NY, NK = 2, 4, 2
NZ, NXH = 16, 2
N_CTX = NX * NY * NK
BLK = 128
BACK = 8
TOK = 64
FEAT = 448
NT = (((1,), (1,)), ((), ()))

score_scale = (1.0 + 0.1 * math.log(40.0)) ** 2 / math.sqrt(192.0)
masked_score = -1e30


class Place:
    def __init__(self):
        self.c = lax.axis_index("ctx")
        self.e = lax.axis_index("ep")
        self.k = lax.rem(self.c, NK)
        self.y = lax.rem(self.c // NK, NY)
        self.x = self.c // (NK * NY)
        self.z = self.e // NXH
        self.h = lax.rem(self.e, NXH)

    def ctx(self, dx, dy, dk):
        x = lax.rem(self.x + dx + NX, NX)
        y = lax.rem(self.y + dy + NY, NY)
        k = lax.rem(self.k + dk + NK, NK)
        return (x * NY + y) * NK + k

    def ep(self, dz, dh):
        z = lax.rem(self.z + dz + NZ, NZ)
        h = lax.rem(self.h + dh + NXH, NXH)
        return z * NXH + h


def remote(src, dst, send, recv, device):
    return pltpu.make_async_remote_copy(
        src_ref=src, dst_ref=dst, send_sem=send, recv_sem=recv,
        device_id=device, device_id_type=pl.DeviceIdType.MESH,
    )


def entry_barrier(devices):
    barrier = pltpu.get_barrier_semaphore()
    for device in devices:
        pl.semaphore_signal(barrier, inc=1, device_id=device, device_id_type=pl.DeviceIdType.MESH)
    pl.semaphore_wait(barrier, len(devices))


CHIPS = [(dx, dy) for dy in (2, 1, 3, 0) for dx in (1, 0) if (dx, dy) != (0, 0)]


def attention_kernel(
    q_ref, lat_ref, doc_ref, wuv_ref, wo_ref, hid_ref, out_ref,
    kt, qs, allow, hv, rr, rl, sr, sl, pr, plft, xs, xr,
    lat_send, lat_recv, hv_send, hv_fwd, hv_recv, zr_send, zr_recv, zl_send, zl_recv, x_sem,
):
    at = Place()
    c, e, z, h = at.c, at.e, at.z, at.h
    peers = [(lax.rem(c + i, N_CTX), e) for i in range(1, N_CTX)]
    right, left, cross = (c, at.ep(1, 0)), (c, at.ep(-1, 0)), (c, at.ep(0, 1))
    entry_barrier(peers + [right, left, cross])

    def latent_copy(d, target):
        return remote(lat_ref, kt.at[:, pl.ds(d * BLK, BLK)], lat_send.at[d - 1], lat_recv.at[d - 1], target)

    for d in range(BACK, 0, -1):
        @pl.when(c + d < N_CTX)
        def _():
            latent_copy(d, (lax.rem(c + d, N_CTX), e)).start()

    kt[:, 0:BLK] = lat_ref[...]
    for n in range(HEADS_DEV):
        qs[n] = q_ref[:, n * KW:(n + 1) * KW]
    own = jnp.broadcast_to(doc_ref[pl.ds(c, 1), :].astype(jnp.float32), (BLK, BLK))
    query_doc = own.T
    rows = lax.broadcasted_iota(jnp.int32, (BLK, BLK), 0)
    cols = lax.broadcasted_iota(jnp.int32, (BLK, BLK), 1)
    allow[:, 0:BLK] = jnp.where((cols <= rows) & (own == query_doc), 1.0, 0.0)
    for d in range(1, BACK + 1):
        key_doc = doc_ref[pl.ds(lax.rem(c - d + N_CTX, N_CTX), 1), :].astype(jnp.float32)
        key_doc = jnp.where(c - d >= 0, key_doc, -1.0)
        allow[:, d * BLK:(d + 1) * BLK] = jnp.where(key_doc == query_doc, 1.0, 0.0)

    for d in range(1, BACK + 1):
        @pl.when(c - d >= 0)
        def _():
            latent_copy(d, (c, e)).wait_recv()

        @pl.when(c - d < 0)
        def _():
            kt[:, pl.ds(d * BLK, BLK)] = jnp.zeros((KW, BLK), jnp.bfloat16)

    @pl.loop(0, HEADS_DEV)
    def _(n):
        allowed = allow[...] > 0.5
        scores = jnp.dot(qs[n], kt[...], preferred_element_type=jnp.float32) * score_scale
        scores = jnp.where(allowed, scores, masked_score)
        peak = jnp.max(scores, axis=1, keepdims=True)
        probs = jnp.where(allowed, jnp.exp(scores - peak), 0.0)
        total = jnp.sum(probs, axis=1, keepdims=True)
        mixed = lax.dot_general(probs.astype(jnp.bfloat16), kt[0:KVL, :], NT, preferred_element_type=jnp.float32)
        context = (mixed / total).astype(jnp.bfloat16)
        value = jnp.dot(context, wuv_ref[n], preferred_element_type=jnp.float32)
        hv[c, :, pl.ds(pl.multiple_of(n * VDIM, VDIM), VDIM)] = value.astype(jnp.bfloat16)

    def value_copy(slot, send, target):
        return remote(hv.at[slot], hv.at[slot], send, hv_recv.at[slot], target)

    for i, (dx, dy) in enumerate(CHIPS):
        value_copy(c, hv_send.at[i], (at.ctx(dx, dy, 0), e)).start()
    mate = (at.ctx(0, 0, 1), e)
    value_copy(c, hv_send.at[7], mate).start()
    for i, (dx, dy) in reversed(list(enumerate(CHIPS))):
        slot = at.ctx(-dx, -dy, 0)
        value_copy(slot, hv_fwd.at[i], mate).wait_recv()
        value_copy(slot, hv_fwd.at[i], mate).start()
    value_copy(at.ctx(0, 0, 1), hv_send.at[7], mate).wait_recv()
    for i, (dx, dy) in reversed(list(enumerate(CHIPS))):
        slot = at.ctx(-dx, -dy, 1)
        value_copy(slot, hv_fwd.at[i], mate).wait_recv()

    def chunk(t):
        return lax.dot_general(hv[t], wo_ref[...], NT, preferred_element_type=jnp.float32)

    theirs = pl.multiple_of((1 - h) * TOK, TOK)
    mine = pl.multiple_of(h * TOK, TOK)

    def hop(rightward, s, half, start):
        if rightward:
            return remote(sr.at[s, pl.ds(start, TOK)], rr.at[s, pl.ds(start, TOK)],
                          zr_send.at[2 * s + half], zr_recv.at[2 * s + half], right)
        return remote(sl.at[s, pl.ds(start, TOK)], rl.at[s, pl.ds(start, TOK)],
                      zl_send.at[2 * s + half], zl_recv.at[2 * s + half], left)

    for s in range(8):
        pr[...] = chunk(lax.rem(z + 8 - s, NZ))
        if s < 7:
            plft[...] = chunk(lax.rem(z + 9 + s, NZ))
        for half, start in ((0, theirs), (1, mine)):
            here = pl.ds(start, TOK)
            value = pr[here, :]
            if s > 0:
                hop(True, s - 1, half, start).wait_recv()
                value = value + rr[s - 1, here, :].astype(jnp.float32)
            sr[s, here, :] = value.astype(jnp.bfloat16)
            hop(True, s, half, start).start()
            if s < 7:
                value = plft[here, :]
                if s > 0:
                    hop(False, s - 1, half, start).wait_recv()
                    value = value + rl[s - 1, here, :].astype(jnp.float32)
                sl[s, here, :] = value.astype(jnp.bfloat16)
                hop(False, s, half, start).start()
    pr[...] = chunk(z)
    for half, start in ((0, theirs), (1, mine)):
        here = pl.ds(start, TOK)
        hop(False, 6, half, start).wait_recv()
        value = pr[here, :] + rl[6, here, :].astype(jnp.float32)
        hop(True, 7, half, start).wait_recv()
        value = value + rr[7, here, :].astype(jnp.float32)
        if half == 0:
            xs[...] = value.astype(jnp.bfloat16)
            swap = remote(xs, xr, x_sem.at[0], x_sem.at[1], cross)
            swap.start()
        else:
            swap.wait_recv()
            out_ref[...] = hid_ref[...].astype(jnp.float32) + (value + xr[...].astype(jnp.float32))

    swap.wait_send()
    for d in range(BACK, 0, -1):
        @pl.when(c + d < N_CTX)
        def _():
            latent_copy(d, (c, e)).wait_send()
    for i in range(len(CHIPS)):
        value_copy(c, hv_send.at[i], mate).wait_send()
        value_copy(c, hv_fwd.at[i], mate).wait_send()
    value_copy(c, hv_send.at[7], mate).wait_send()
    for s in range(8):
        for half, start in ((0, theirs), (1, mine)):
            hop(True, s, half, start).wait_send()
            if s < 7:
                hop(False, s, half, start).wait_send()


def attention_part(queries, latent, doc_ids, w_uv, w_out, hidden_in):
    vmem = pl.BlockSpec(memory_space=pltpu.VMEM)
    bf, f32 = jnp.bfloat16, jnp.float32
    dma = pltpu.SemaphoreType.DMA
    return pl.pallas_call(
        attention_kernel,
        out_shape=jax.ShapeDtypeStruct((TOK, FEAT), f32),
        in_specs=[vmem] * 6,
        out_specs=vmem,
        scratch_shapes=[
            pltpu.VMEM((KW, (BACK + 1) * BLK), bf),
            pltpu.VMEM((HEADS_DEV, BLK, KW), bf),
            pltpu.VMEM((BLK, (BACK + 1) * BLK), f32),
            pltpu.VMEM((N_CTX, BLK, HEADS_DEV * VDIM), bf),
            pltpu.VMEM((8, BLK, FEAT), bf),
            pltpu.VMEM((7, BLK, FEAT), bf),
            pltpu.VMEM((8, BLK, FEAT), bf),
            pltpu.VMEM((7, BLK, FEAT), bf),
            pltpu.VMEM((BLK, FEAT), f32),
            pltpu.VMEM((BLK, FEAT), f32),
            pltpu.VMEM((TOK, FEAT), bf),
            pltpu.VMEM((TOK, FEAT), bf),
            dma((8,)), dma((8,)), dma((8,)), dma((7,)), dma((16,)),
            dma((16,)), dma((16,)), dma((14,)), dma((14,)), dma((2,)),
        ],
        compiler_params=pltpu.CompilerParams(
            collective_id=0, has_side_effects=True, vmem_limit_bytes=48 << 20
        ),
    )(queries, latent.T, doc_ids.reshape(N_CTX, BLK), w_uv, w_out.T, hidden_in)


HALF = 288
SPAN = NZ * TOK
ROWS = 2 * HALF
PIECE = ROWS // NY
QUART = 256
FF = 1024
TOP = 8
EP_STEPS = [(dz, dh) for dz in range(NZ) for dh in range(NXH) if (dz, dh) != (0, 0)]


def silu(v):
    return v / (1.0 + jnp.exp(-v))


def moe_kernel(
    res_ref, gain_ref, ids_ref, wts_ref, wg_ref, wu_ref, wd_ref, out_ref,
    route, tabs, s_own, s_mate, s_far, t_own, t_mate, w_col, r_col, sq, rs_all, r_rows, xs, picked, far_in,
    g, rk, yb, yf, ys, xsend, xb, act, yw, y_far, prod, rr, rl, sr, sl,
    route_send, route_recv, sq_send, sq_recv, r_send, r_recv, ar_send, ar_recv, al_send, al_recv, px_sem,
    k_send, k_recv, y_send, y_recv, gx_sem, a_send, a_recv, bx_sem, zr_send, zr_recv, zl_send, zl_recv,
):
    bf, f32 = jnp.bfloat16, jnp.float32
    at = Place()
    c, e, x, y, k, z, h = at.c, at.e, at.x, at.y, at.k, at.z, at.h
    right, left, cross = (c, at.ep(1, 0)), (c, at.ep(-1, 0)), (c, at.ep(0, 1))
    mate, side = (at.ctx(0, 0, 1), e), (at.ctx(1, 0, 0), e)
    ahead, behind = (at.ctx(0, 1, 0), e), (at.ctx(0, -1, 0), e)
    ep_peers = [(c, at.ep(dz, dh)) for dz, dh in EP_STEPS]
    ctx_peers = [(lax.rem(c + i, N_CTX), e) for i in range(1, N_CTX)]
    entry_barrier(ep_peers + ctx_peers)

    def route_copy(i, slot, target):
        return remote(route.at[slot], route.at[slot], route_send.at[i], route_recv.at[slot], target)

    route[e, 0:8, :] = ids_ref[...].astype(f32)
    route[e, 8:16, :] = wts_ref[...]
    for i in range(len(EP_STEPS)):
        route_copy(i, e, ep_peers[i]).start()

    res = res_ref[...]
    part = jnp.broadcast_to(jnp.sum(res * res, axis=1, keepdims=True), (TOK, 128))
    sq[c] = part.T[0:8, :]

    def sq_copy(i, slot, target):
        return remote(sq.at[slot], sq.at[slot], sq_send.at[i], sq_recv.at[slot], target)

    for i in range(1, N_CTX):
        sq_copy(i - 1, c, ctx_peers[i - 1]).start()

    xs[z] = (res * gain_ref[...]).astype(bf)

    def pass_on(rightward, s):
        slot = lax.rem(z + NZ - s, NZ) if rightward else lax.rem(z + s, NZ)
        if rightward:
            return remote(xs.at[slot], xs.at[slot], ar_send.at[s], ar_recv.at[s], right)
        return remote(xs.at[slot], xs.at[slot], al_send.at[s], al_recv.at[s], left)

    def arrived(rightward, s):
        slot = lax.rem(z + NZ - s - 1, NZ) if rightward else lax.rem(z + s + 1, NZ)
        if rightward:
            return remote(xs.at[slot], xs.at[slot], ar_send.at[s], ar_recv.at[s], right)
        return remote(xs.at[slot], xs.at[slot], al_send.at[s], al_recv.at[s], left)

    pass_on(True, 0).start()
    pass_on(False, 0).start()

    for dz, dh in EP_STEPS:
        slot = at.ep(dz, dh)
        route_copy(0, slot, mate).wait_recv()
    mate_e = at.ep(0, 1)
    for n in range(NZ):
        near = route[n * NXH + h]
        far = route[n * NXH + (1 - h)]
        lanes = slice(n * TOK, (n + 1) * TOK)
        own_hit = jnp.where(near[0:8] == e.astype(f32), 1.0, 0.0)
        mate_hit = jnp.where(near[0:8] == mate_e.astype(f32), 1.0, 0.0)
        far_hit = jnp.where(far[0:8] == e.astype(f32), 1.0, 0.0)
        tabs[0:1, lanes] = jnp.sum(own_hit, axis=0, keepdims=True)
        tabs[1:2, lanes] = jnp.sum(mate_hit, axis=0, keepdims=True)
        tabs[2:3, lanes] = jnp.sum(far_hit, axis=0, keepdims=True)
        tabs[3:4, lanes] = jnp.sum(own_hit * near[8:16], axis=0, keepdims=True)
        tabs[4:5, lanes] = jnp.sum(far_hit * far[8:16], axis=0, keepdims=True)
        tabs[5:8, lanes] = jnp.zeros((3, TOK), f32)
    tri = jnp.where(
        lax.broadcasted_iota(jnp.int32, (128, 128), 0) < lax.broadcasted_iota(jnp.int32, (128, 128), 1), 1.0, 0.0
    ).astype(bf)
    base = jnp.zeros((8, 1), f32)
    w_own = jnp.zeros((HALF, 1), f32)
    w_far = jnp.zeros((HALF, 1), f32)
    for n in range(SPAN // 128):
        lanes = slice(n * 128, (n + 1) * 128)
        hit = tabs[:, lanes]
        rank = jnp.dot(hit.astype(bf), tri, preferred_element_type=f32) + base
        base = base + jnp.sum(hit, axis=1, keepdims=True)
        slot = jnp.where(hit > 0.5, rank, -1.0)
        row = lax.broadcasted_iota(jnp.int32, (HALF, 128), 0).astype(f32)
        pick_own = jnp.where(slot[0:1] == row, 1.0, 0.0)
        pick_far = jnp.where(slot[2:3] == row, 1.0, 0.0)
        s_own[:, lanes] = pick_own.astype(bf)
        s_mate[:, lanes] = jnp.where(slot[1:2] == row, 1.0, 0.0).astype(bf)
        s_far[:, lanes] = pick_far.astype(bf)
        w_own = w_own + jnp.sum(pick_own * tabs[3:4, lanes], axis=1, keepdims=True)
        w_far = w_far + jnp.sum(pick_far * tabs[4:5, lanes], axis=1, keepdims=True)
        col = lax.broadcasted_iota(jnp.int32, (128, HALF), 1).astype(f32)
        own_col = jnp.broadcast_to(slot[0:1], (128, 128)).T[:, 0:1]
        mate_col = jnp.broadcast_to(slot[1:2], (128, 128)).T[:, 0:1]
        t_own[lanes, :] = jnp.where(own_col == col, 1.0, 0.0).astype(bf)
        t_mate[lanes, :] = jnp.where(mate_col == col, 1.0, 0.0).astype(bf)
    w_col[0:HALF, :] = jnp.broadcast_to(w_own, (HALF, 128))
    w_col[HALF:ROWS, :] = jnp.broadcast_to(w_far, (HALF, 128))

    for i in range(1, N_CTX):
        sq_copy(0, lax.rem(c + i, N_CTX), mate).wait_recv()
    total = sq[0]
    for i in range(1, N_CTX):
        total = total + sq[i]
    rs_all[e] = lax.rsqrt(total / D + 1e-06)

    def r_copy(i, slot, target):
        return remote(rs_all.at[slot], rs_all.at[slot], r_send.at[i], r_recv.at[slot], target)

    for i in range(len(EP_STEPS)):
        r_copy(i, e, ep_peers[i]).start()

    for s in range(8):
        arrived(True, s).wait_recv()
        if s < 7:
            pass_on(True, s + 1).start()
            arrived(False, s).wait_recv()
            if s < 6:
                pass_on(False, s + 1).start()

    flat = xs[...].reshape(SPAN, FEAT)
    picked[HALF:ROWS, :] = jnp.dot(s_mate[...], flat, preferred_element_type=f32).astype(bf)
    swap = remote(picked.at[pl.ds(HALF, HALF)], far_in, px_sem.at[0], px_sem.at[1], cross)
    swap.start()
    picked[0:HALF, :] = jnp.dot(s_own[...], flat, preferred_element_type=f32).astype(bf)

    for dz, dh in EP_STEPS:
        r_copy(0, at.ep(dz, dh), mate).wait_recv()
    for n in range(NZ):
        lanes = slice(n * TOK, (n + 1) * TOK)
        r_rows[0:1, lanes] = rs_all[n * NXH + h][0:1, 0:TOK]
        r_rows[1:2, lanes] = rs_all[n * NXH + (1 - h)][0:1, 0:TOK]
    r_col[0:HALF, :] = jnp.broadcast_to(
        jnp.sum(s_own[...].astype(f32) * r_rows[0:1, :], axis=1, keepdims=True), (HALF, 128))
    r_col[HALF:ROWS, :] = jnp.broadcast_to(
        jnp.sum(s_far[...].astype(f32) * r_rows[1:2, :], axis=1, keepdims=True), (HALF, 128))

    def terms(source, first, q):
        rows = pl.ds(first, HALF)
        cols = pl.ds(pl.multiple_of(q * QUART, QUART), QUART)
        scale = r_col[rows, 0:1]
        value = source[...] if first else source[0:HALF, :]
        g[q, rows, 0:QUART] = (jnp.dot(value, wg_ref[:, cols], preferred_element_type=f32) * scale).astype(bf)
        g[q, rows, QUART:2 * QUART] = (jnp.dot(value, wu_ref[:, cols], preferred_element_type=f32) * scale).astype(bf)

    def k_copy(xx, first):
        i = 2 * xx + (1 if first else 0)
        return remote(g.at[xx * NK + (1 - k), pl.ds(first, HALF)], rk.at[xx, pl.ds(first, HALF)],
                      k_send.at[i], k_recv.at[i], mate)

    for source, first in ((picked, 0), (far_in, HALF)):
        if first:
            swap.wait_recv()
        for xx in range(NX):
            terms(source, first, xx * NK + (1 - k))
            k_copy(xx, first).start()
        for xx in range(NX):
            terms(source, first, xx * NK + k)

    for first in (0, HALF):
        for xx in range(NX):
            k_copy(xx, first).wait_recv()

    def pair_sum(xx, yy):
        rows = pl.ds(pl.multiple_of(yy * PIECE, 16), PIECE)
        return g[xx * NK + k, rows, :].astype(f32) + rk[xx, rows, :].astype(f32)

    y_up, y_down, y_over = lax.rem(y + 1, NY), lax.rem(y + 3, NY), lax.rem(y + 2, NY)

    def y_copy(i):
        dst = [yb.at[0], yb.at[1], yf.at[0, 1], yf.at[1, 0], yf.at[0, 0], yf.at[1, 1]][i]
        return remote(ys.at[i], dst, y_send.at[i], y_recv.at[i], ahead if i % 2 == 0 else behind)

    def y_put(i, value):
        ys[i] = value.astype(bf)
        y_copy(i).start()

    y_put(0, pair_sum(0, y_over))
    y_put(1, pair_sum(1, y_over))
    y_put(2, pair_sum(1, y_up))
    y_put(3, pair_sum(0, y_down))
    y_copy(0).wait_recv()
    y_put(4, pair_sum(0, y_up) + yb[0].astype(f32))
    y_copy(1).wait_recv()
    y_put(5, pair_sum(1, y_down) + yb[1].astype(f32))
    for i in range(2, 6):
        y_copy(i).wait_recv()

    def full_sum(xx):
        return pair_sum(xx, y) + yf[0, xx].astype(f32) + yf[1, xx].astype(f32)

    xsend[...] = full_sum(1 - x).astype(bf)
    gx = remote(xsend, xb, gx_sem.at[0], gx_sem.at[1], side)
    gx.start()
    sums = full_sum(x)
    gx.wait_recv()
    sums = sums + xb[...].astype(f32)
    done = (silu(sums[:, 0:QUART]) * sums[:, QUART:2 * QUART]).astype(bf)

    def spot(dx, dy, dk):
        xx, yy, kk = lax.rem(x + dx, NX), lax.rem(y + dy + NY, NY), lax.rem(k + dk, NK)
        ref = act.at[pl.ds(pl.multiple_of(yy * PIECE, 16), PIECE), pl.ds(pl.multiple_of((xx * NK + kk) * QUART, QUART), QUART)]
        return ref, (xx * NY + yy) * NK + kk

    act[pl.ds(pl.multiple_of(y * PIECE, 16), PIECE), pl.ds(pl.multiple_of((x * NK + k) * QUART, QUART), QUART)] = done
    sent = []

    def give(dx, dy, target):
        ref, slot = spot(dx, dy, 0)
        copy = remote(ref, ref, a_send.at[len(sent)], a_recv.at[slot], target)
        copy.start()
        sent.append(copy)

    def take(dx, dy, dk):
        ref, slot = spot(dx, dy, dk)
        remote(ref, ref, a_send.at[0], a_recv.at[slot], mate).wait_recv()

    for target in (side, ahead, behind, mate):
        give(0, 0, target)
    take(1, 0, 0)
    for target in (ahead, behind, mate):
        give(1, 0, target)
    for dx in range(NX):
        for dy in (-1, 1):
            take((dx + 0), dy, 0)
            if (dx, dy) == (0, -1):
                give(0, -1, ahead)
            if (dx, dy) == (1, 1):
                give(1, 1, behind)
            give(dx, dy, mate)
    for dx in range(NX):
        take(dx, 2, 0)
        give(dx, 2, mate)
    for dy in (0, -1, 1, 2):
        for dx in range(NX):
            take(dx, dy, 1)

    def down(first):
        value = lax.dot_general(act[first:first + HALF, :], wd_ref[...], NT, preferred_element_type=f32)
        yw[first:first + HALF, :] = (value * w_col[first:first + HALF, 0:1]).astype(bf)

    down(HALF)
    back = remote(yw.at[pl.ds(HALF, HALF)], y_far, bx_sem.at[0], bx_sem.at[1], cross)
    back.start()
    down(0)
    prod[...] = jnp.dot(t_own[...], yw[0:HALF, :], preferred_element_type=f32)
    back.wait_recv()
    prod[...] += jnp.dot(t_mate[...], y_far[...], preferred_element_type=f32)

    def hop(rightward, s, half):
        part = pl.ds(half * 32, 32)
        if rightward:
            return remote(sr.at[s, part], rr.at[s, part], zr_send.at[2 * s + half], zr_recv.at[2 * s + half], right)
        return remote(sl.at[s, part], rl.at[s, part], zl_send.at[2 * s + half], zl_recv.at[2 * s + half], left)

    def block(t, half):
        return prod[pl.ds(pl.multiple_of(t * TOK + half * 32, 32), 32), :]

    for s in range(8):
        for half in range(2):
            part = pl.ds(half * 32, 32)
            value = block(lax.rem(z + 8 - s, NZ), half)
            if s > 0:
                hop(True, s - 1, half).wait_recv()
                value = value + rr[s - 1, part, :].astype(f32)
            sr[s, part, :] = value.astype(bf)
            hop(True, s, half).start()
            if s < 7:
                value = block(lax.rem(z + 9 + s, NZ), half)
                if s > 0:
                    hop(False, s - 1, half).wait_recv()
                    value = value + rl[s - 1, part, :].astype(f32)
                sl[s, part, :] = value.astype(bf)
                hop(False, s, half).start()
    for half in range(2):
        part = pl.ds(half * 32, 32)
        hop(False, 6, half).wait_recv()
        value = block(z, half) + rl[6, part, :].astype(f32)
        hop(True, 7, half).wait_recv()
        value = value + rr[7, part, :].astype(f32)
        out_ref[part, :] = (res_ref[part, :] + value).astype(bf)

    for i in range(len(EP_STEPS)):
        route_copy(i, e, mate).wait_send()
        r_copy(i, e, mate).wait_send()
    for i in range(1, N_CTX):
        sq_copy(i - 1, c, mate).wait_send()
    for s in range(8):
        pass_on(True, s).wait_send()
        if s < 7:
            pass_on(False, s).wait_send()
        for half in range(2):
            hop(True, s, half).wait_send()
            if s < 7:
                hop(False, s, half).wait_send()
    swap.wait_send()
    for first in (0, HALF):
        for xx in range(NX):
            k_copy(xx, first).wait_send()
    for i in range(6):
        y_copy(i).wait_send()
    gx.wait_send()
    for copy in sent:
        copy.wait_send()
    back.wait_send()


def moe_part(residual, norm_gain, route_ids, route_weights, w_gate, w_up, w_down):
    vmem = pl.BlockSpec(memory_space=pltpu.VMEM)
    bf, f32 = jnp.bfloat16, jnp.float32
    dma = pltpu.SemaphoreType.DMA
    shapes = [
        ((32, 16, TOK), f32), ((8, SPAN), f32),
        ((HALF, SPAN), bf), ((HALF, SPAN), bf), ((HALF, SPAN), bf), ((SPAN, HALF), bf), ((SPAN, HALF), bf),
        ((ROWS, 128), f32), ((ROWS, 128), f32), ((N_CTX, 8, TOK), f32), ((32, 8, TOK), f32), ((2, SPAN), f32),
        ((NZ, TOK, FEAT), bf), ((ROWS, FEAT), bf), ((HALF, FEAT), bf),
        ((4, ROWS, 2 * QUART), bf), ((NX, ROWS, 2 * QUART), bf), ((2, PIECE, 2 * QUART), bf),
        ((2, 2, PIECE, 2 * QUART), bf), ((6, PIECE, 2 * QUART), bf), ((PIECE, 2 * QUART), bf),
        ((PIECE, 2 * QUART), bf), ((ROWS, FF), bf), ((ROWS, FEAT), bf), ((HALF, FEAT), bf), ((SPAN, FEAT), f32),
        ((8, TOK, FEAT), bf), ((7, TOK, FEAT), bf), ((8, TOK, FEAT), bf), ((7, TOK, FEAT), bf),
    ]
    counts = [31, 32, 15, 16, 31, 32, 8, 8, 7, 7, 2, 4, 4, 6, 6, 2, 17, 16, 2, 16, 16, 14, 14]
    return pl.pallas_call(
        moe_kernel,
        out_shape=jax.ShapeDtypeStruct((TOK, FEAT), bf),
        in_specs=[vmem] * 7,
        out_specs=vmem,
        scratch_shapes=[pltpu.VMEM(s, d) for s, d in shapes] + [dma((n,)) for n in counts],
        compiler_params=pltpu.CompilerParams(
            collective_id=1, has_side_effects=True, vmem_limit_bytes=48 << 20
        ),
    )(residual, norm_gain.reshape(1, FEAT), route_ids.T, route_weights.T, w_gate[0], w_up[0], w_down[0].T)


def shards(
    queries, latent, doc_ids, w_uv, w_out, hidden_in, norm_gain, route_ids, route_weights, w_gate, w_up, w_down,
):
    residual = attention_part(queries, latent, doc_ids, w_uv, w_out, hidden_in)
    return moe_part(residual, norm_gain, route_ids, route_weights, w_gate, w_up, w_down)


def solution(mesh):
    return jax.shard_map(
        shards,
        mesh=mesh,
        in_specs=(
            P("ctx", "ep"), P("ctx", None), P(), P("ep", None, None), P("ep", "ctx"), P("ep", "ctx"),
            P("ctx"), P("ep", None), P("ep", None),
            P("ep", "ctx", None), P("ep", "ctx", None), P("ep", None, "ctx"),
        ),
        out_specs=P("ep", "ctx"),
        check_vma=False,
    )
```
